32 devices in a mesh: layer: 4 (over z), dp: 8 (over y, x, core).
Axes of the slice: x: 2, y: 2, z: 4, core: 2. Of those that a mesh axis runs over, the one named last changes fastest.
Arguments:
- inputs: bfloat16 [4, 8192, 768], P('layer', 'dp'), may hold values from -6 to 6
- cotangent: bfloat16 [4, 8192, 768], P('layer', 'dp'), may hold values from -6 to 6
- drop_mask: int32 [4, 16, 8], P('layer', 'dp'), may hold values 0 or 1
- doc_len: int32 [4, 16, 8], P('layer', 'dp'), may hold values from 1 to 128, 512 in all within a row
- w_query: bfloat16 [4, 768, 768], P('layer'), may hold values from -0.21875 to 0.21875
- b_query: bfloat16 [4, 768], P('layer'), may hold values from -4 to 4
- w_key: bfloat16 [4, 768, 768], P('layer'), may hold values from -0.21875 to 0.21875
- w_value: bfloat16 [4, 768, 768], P('layer'), may hold values from -0.21875 to 0.21875
- b_value: bfloat16 [4, 768], P('layer'), may hold values from -4 to 4
- w_attn: bfloat16 [4, 768, 768], P('layer'), may hold values from -0.875 to 0.875
- b_attn: bfloat16 [4, 768], P('layer'), may hold values from -4 to 4
- gain_one: bfloat16 [4, 768], P('layer'), may hold values from 0.099609375 to 1.8984375
- shift_one: bfloat16 [4, 768], P('layer'), may hold values from -4 to 4
- w_in: bfloat16 [4, 768, 3072], P('layer'), may hold values from -0.21875 to 0.21875
- b_in: bfloat16 [4, 3072], P('layer'), may hold values from -4 to 4
- w_out: bfloat16 [4, 3072, 768], P('layer'), may hold values from -0.109375 to 0.109375
- b_out: bfloat16 [4, 768], P('layer'), may hold values from -4 to 4
- gain_two: bfloat16 [4, 768], P('layer'), may hold values from 0.099609375 to 1.8984375
- shift_two: bfloat16 [4, 768], P('layer'), may hold values from -4 to 4
Outputs:
- out: bfloat16 [4, 8192, 768], P('layer', 'dp')
- grad_inputs: bfloat16 [4, 8192, 768], P('layer', 'dp')
- grad_w_query: float32 [4, 768, 768], P('layer')
- grad_b_query: float32 [4, 768], P('layer')
- grad_w_key: float32 [4, 768, 768], P('layer')
- grad_w_value: float32 [4, 768, 768], P('layer')
- grad_b_value: float32 [4, 768], P('layer')
- grad_w_attn: float32 [4, 768, 768], P('layer')
- grad_b_attn: float32 [4, 768], P('layer')
- grad_gain_one: float32 [4, 768], P('layer')
- grad_shift_one: float32 [4, 768], P('layer')
- grad_w_in: float32 [4, 768, 3072], P('layer')
- grad_b_in: float32 [4, 3072], P('layer')
- grad_w_out: float32 [4, 3072, 768], P('layer')
- grad_b_out: float32 [4, 768], P('layer')
- grad_gain_two: float32 [4, 768], P('layer')
- grad_shift_two: float32 [4, 768], P('layer')
The draws below stay inside these ranges and needn't reach their ends.
Inputs may be any that keep to these rules, and one draw needn't show every extreme that they name: Slots of devices with an even index within a layer group hold one document: for them only entry 0 of drop_mask is read and doc_len is not read. The lengths of each slot sum to 512.
All inputs are finite; a program needn't handle non-finite values. No bound on the sum of `drop_mask` on one device may be relied on, other than what follows from the above.
Results may differ from the reference program's by a relative error of at most 0.018.
Values may be sent and summed in bfloat16 or wider, within the bound.
A program may use at most 192 MiB of HBM per device.

```python
import math
import jax
import jax.numpy as jnp
import numpy as np
from jax import lax

D = 768
HEADS = 12
HD = 64
FF = 3072
SEQ = 512
DOC_MAX = 128
DOCS = 8
SLOTS_DEV = 2
LAYERS = 4
SLOTS = 16
TOKENS = 8192


def with_ends(drawn, key, smallest, top_value):
    spot = [jax.random.randint(jax.random.fold_in(key, axis), (), 0, length) for axis, length in enumerate(drawn.shape)]
    longest = drawn.shape.index(max(drawn.shape))
    beside = spot[:longest] + [(spot[longest] + 1) % drawn.shape[longest]] + spot[longest + 1:]
    return drawn.at[tuple(spot)].set(smallest).at[tuple(beside)].set(top_value)


def level_of(stream_key, extent, cuts, least, high):
    def one(dim, shards_of):
        steps = jax.random.uniform(jax.random.fold_in(jax.random.fold_in(stream_key, 6), dim), (shards_of,), jnp.float32, least / len(cuts), high / len(cuts))
        return jnp.repeat(jnp.exp(steps), extent[dim] // shards_of).reshape((-1,) + (1,) * (len(extent) - dim - 1))

    level = one(*cuts[0])
    for cut in cuts[1:]:
        level = level * one(*cut)
    return level


def split_up(amount, total, reach, lean):
    loads = [(1 << 20) // math.isqrt(rank ** lean) + 1 for rank in range(2, amount + 1)]
    spare, counts = total - reach - (amount - 1), [1] * (amount - 1)
    while spare > 0:
        movable = [i for i in range(amount - 1) if counts[i] < reach]
        mass, budget = sum([loads[i] for i in movable]), spare
        for i in movable:
            more = min(reach - counts[i], max(1, budget * loads[i] // mass), spare)
            counts[i] = counts[i] + more
            spare = spare - more
    return np.array([reach] + counts)


def uneven_parts(rng, number_of, total, limit, skew):
    if number_of == 2:
        one = jax.random.randint(rng, (), max(1, total - limit), min(limit, total - 1) + 1)
        return jnp.stack([one, total - one])
    sizes = jnp.asarray(split_up(number_of, total, limit, skew), jnp.int32)
    pairs = (number_of - 1) // 2
    donor, taker = sizes[1:1 + 2 * pairs:2], sizes[2:2 + 2 * pairs:2]
    slack = jnp.minimum(donor - 1, limit - taker)
    shifted = jax.random.randint(jax.random.fold_in(rng, 1), (pairs,), 0, 1 << 20) % (slack + 1)
    sizes = sizes.at[1:1 + 2 * pairs:2].set(donor - shifted).at[2:2 + 2 * pairs:2].set(taker + shifted)
    return sizes[jax.random.permutation(jax.random.fold_in(rng, 2), number_of)]


def normal_values(key, extent, deviation, reach, pieces=(), kind=jnp.bfloat16):
    values = jax.random.normal(key, extent, jnp.float32) * deviation
    if len(pieces) > 0:
        values = level_of(key, extent, pieces, -0.22, 0.18) * values
    return jnp.clip(values, min=-reach, max=reach).astype(kind)


def setup_inputs(seed: int = 0) -> dict:
    key_list = jax.random.split(jax.random.key(seed), 20)
    inputs = normal_values(key_list[0], (LAYERS, TOKENS, D), 1.0, 6.0, ((0, 4), (1, 8)))
    cotangent = normal_values(key_list[1], (LAYERS, TOKENS, D), 1.0, 6.0, ((0, 4), (1, 8)))
    drop_mask = with_ends((jax.random.randint(key_list[2], (LAYERS, SLOTS, DOCS), 0, 4) < 1).astype(jnp.int32), jax.random.fold_in(key_list[2], 1), 0, 1)
    doc_len = jax.vmap(lambda own: uneven_parts(own, DOCS, SEQ, DOC_MAX, 2))(jax.random.split(key_list[3], LAYERS * SLOTS)).reshape((LAYERS, SLOTS, DOCS)).astype(jnp.int32)
    w_query = normal_values(key_list[4], (LAYERS, D, D), D ** -0.5, 0.21875, ((0, 4),))
    b_query = normal_values(key_list[5], (LAYERS, D), 0.3, 4.0, ((0, 4),))
    w_key = normal_values(key_list[6], (LAYERS, D, D), D ** -0.5, 0.21875, ((0, 4),))
    w_value = normal_values(key_list[7], (LAYERS, D, D), D ** -0.5, 0.21875, ((0, 4),))
    b_value = normal_values(key_list[8], (LAYERS, D), 0.3, 4.0, ((0, 4),))
    w_attn = normal_values(key_list[9], (LAYERS, D, D), (D // 16) ** -0.5, 0.875, ((0, 4),))
    b_attn = normal_values(key_list[10], (LAYERS, D), 0.3, 4.0, ((0, 4),))
    gain_one = jnp.clip(1.0 + 0.18 * jax.random.normal(key_list[11], (LAYERS, D), jnp.float32), 0.099609375, 1.8984375).astype(jnp.bfloat16)
    shift_one = normal_values(key_list[12], (LAYERS, D), 0.3, 4.0, ((0, 4),))
    w_in = normal_values(key_list[13], (LAYERS, D, FF), D ** -0.5, 0.21875, ((0, 4),))
    b_in = normal_values(key_list[14], (LAYERS, FF), 0.3, 4.0, ((0, 4),))
    w_out = normal_values(key_list[15], (LAYERS, FF, D), FF ** -0.5, 0.109375, ((0, 4),))
    b_out = normal_values(key_list[16], (LAYERS, D), 0.3, 4.0, ((0, 4),))
    gain_two = jnp.clip(1.0 + 0.18 * jax.random.normal(key_list[17], (LAYERS, D), jnp.float32), 0.099609375, 1.8984375).astype(jnp.bfloat16)
    shift_two = normal_values(key_list[18], (LAYERS, D), 0.3, 4.0, ((0, 4),))
    return dict(inputs=inputs, cotangent=cotangent, drop_mask=drop_mask, doc_len=doc_len, w_query=w_query, b_query=b_query, w_key=w_key, w_value=w_value, b_value=b_value, w_attn=w_attn, b_attn=b_attn, gain_one=gain_one, shift_one=shift_one, w_in=w_in, b_in=b_in, w_out=w_out, b_out=b_out, gain_two=gain_two, shift_two=shift_two)


@jax.custom_vjp
def low(v):
    return lax.optimization_barrier(v.astype(jnp.bfloat16)).astype(jnp.float32)

@jax.custom_vjp
def low_back(v):
    return v

def low_keep(v):
    return (low(v), None)

def low_pass(kept, grad):
    return (grad,)

def back_keep(v):
    return (v, None)

def back_low(kept, grad):
    return (low(grad),)
low.defvjp(low_keep, low_pass)
low_back.defvjp(back_keep, back_low)

def matmul(left, right):
    return jnp.dot(left, right, precision=lax.Precision.HIGHEST)

def layer_norm(values, gain, shift):
    center = lax.optimization_barrier(jnp.mean(values, axis=-1, keepdims=True))
    centered = values - center
    spread = lax.optimization_barrier(jnp.mean(centered * centered, axis=-1, keepdims=True))
    return centered * lax.rsqrt(spread + 1e-05) * gain + shift

def segments_of(lengths, long_bucket):
    ends = jnp.cumsum(lengths).astype(jnp.int32)
    places = jnp.arange(SEQ, dtype=jnp.int32)
    segment = lax.optimization_barrier(jnp.sum((places[:, None] >= ends[None, :]).astype(jnp.int32), axis=1)).astype(jnp.int32)
    return jnp.where(long_bucket, jnp.zeros_like(segment), segment)

def keep_of(masks, segment):
    chosen = segment[:, None] == jnp.arange(DOCS, dtype=jnp.int32)[None, :]
    dropped = lax.optimization_barrier(jnp.sum(jnp.where(chosen, masks[None, :], 0), axis=1))
    return dropped == 0

def slot_layer(params, tok_rows, segment, keep_rows):
    w_query, b_query, w_key, w_value, b_value, w_attn, b_attn, gain_one, shift_one, w_in, b_in, w_out, b_out, gain_two, shift_two = params
    queries = low(low_back(matmul(tok_rows, w_query) + b_query))
    key_rows = low(low_back(matmul(tok_rows, w_key)))
    values = low(low_back(matmul(tok_rows, w_value) + b_value))
    head_q = queries.reshape(SEQ, HEADS, HD)
    head_k = key_rows.reshape(SEQ, HEADS, HD)
    head_v = values.reshape(SEQ, HEADS, HD)
    scores = low_back(jnp.einsum('qhd,khd->hqk', head_q, head_k, precision=lax.Precision.HIGHEST) * HD ** (-0.5))
    same_doc = segment[:, None] == segment[None, :]
    scores = jnp.where(same_doc[None], scores, -1e+30)
    row_top = lax.optimization_barrier(jnp.max(scores, axis=-1, keepdims=True))
    expo = jnp.exp(scores - row_top)
    probs = low(expo / lax.optimization_barrier(jnp.sum(expo, axis=-1, keepdims=True)))
    mixed = jnp.einsum('hqk,khd->qhd', probs, head_v, precision=lax.Precision.HIGHEST).reshape(SEQ, D)
    mixed = low(low_back(mixed))
    attended = low_back(matmul(mixed, w_attn)) + b_attn
    first = layer_norm(tok_rows + attended, gain_one, shift_one)
    sent = low(low_back(first))
    inner = low(jax.nn.gelu(low_back(matmul(sent, w_in)) + b_in, approximate=False))
    outer = low_back(matmul(inner, w_out)) + b_out
    final = layer_norm(sent + outer, gain_two, shift_two)
    return jnp.where(keep_rows[:, None], final, tok_rows)

def reference(inputs, cotangent, drop_mask, doc_len, w_query, b_query, w_key, w_value, b_value, w_attn, b_attn, gain_one, shift_one, w_in, b_in, w_out, b_out, gain_two, shift_two):
    weights = (w_query, b_query, w_key, w_value, b_value, w_attn, b_attn, gain_one, shift_one, w_in, b_in, w_out, b_out, gain_two, shift_two)
    slot_index = jnp.arange(SLOTS, dtype=jnp.int32)
    long_bucket = slot_index // SLOTS_DEV % 2 == 0
    results = []
    grad_rows_all = []
    grad_lists = [[] for weight in weights]
    for layer_idx in range(LAYERS):
        tok_rows = inputs[layer_idx].astype(jnp.float32).reshape(SLOTS, SEQ, D)
        segments = jax.vmap(segments_of)(doc_len[layer_idx], long_bucket)
        keeps = jax.vmap(keep_of)(drop_mask[layer_idx], segments)
        params = tuple((weight[layer_idx].astype(jnp.float32) for weight in weights))

        def forward(slot_rows, layer_params):
            runner = jax.checkpoint(slot_layer)

            def scan_step(running, slot_item):
                return (running, runner(layer_params, slot_item[0], slot_item[1], slot_item[2]))
            return lax.scan(scan_step, jnp.zeros((), jnp.float32), (slot_rows, segments, keeps))[1]
        final, pull = jax.vjp(forward, tok_rows, params)
        incoming = cotangent[(layer_idx + 1) % LAYERS].astype(jnp.float32).reshape(SLOTS, SEQ, D)
        grad_rows, grad_params = pull(incoming)
        results.append(final.reshape(TOKENS, D).astype(jnp.bfloat16))
        grad_rows_all.append(grad_rows.reshape(TOKENS, D).astype(jnp.bfloat16))
        for position in range(len(weights)):
            grad_lists[position].append(grad_params[position])
    out = jnp.roll(jnp.stack(results), 1, axis=0)
    grad_inputs = jnp.stack(grad_rows_all)
    grads = [jnp.stack(items) for items in grad_lists]
    return (out, grad_inputs, grads[0], grads[1], grads[2], grads[3], grads[4], grads[5], grads[6], grads[7], grads[8], grads[9], grads[10], grads[11], grads[12], grads[13], grads[14])
```

```python
import jax
import jax.numpy as jnp
from jax import lax
from jax.sharding import PartitionSpec as P

HEADS = 12
HD = 64


eps_norm = 1e-05


def shifted(block, axis, distance):
    devices = range(lax.axis_size(axis))
    route = [((i - distance) % len(devices), i) for i in devices]
    return lax.ppermute(block, axis, route)


def norm_parts(values):
    center = jnp.mean(values, axis=-1, keepdims=True)
    centered = values - center
    spread = jnp.mean(centered * centered, axis=-1, keepdims=True)
    scaled = lax.rsqrt(spread + eps_norm)
    return (centered * scaled, scaled)


def norm_back(grad_out, normed, scaled, gain):
    grad_norm = grad_out * gain
    first_mean = jnp.mean(grad_norm, axis=-1, keepdims=True)
    second_mean = jnp.mean(grad_norm * normed, axis=-1, keepdims=True)
    grad_in = scaled * (grad_norm - first_mean - normed * second_mean)
    return (grad_in, jnp.sum(grad_out * normed, axis=0), jnp.sum(grad_out, axis=0))


def row_product(left, right):
    return jnp.einsum("nd,nf->df", left, right, preferred_element_type=jnp.float32)


def back_product(left, right):
    return jnp.einsum("nf,df->nd", left, right, preferred_element_type=jnp.float32)


def gelu_exact(values):
    return jax.nn.gelu(values, approximate=False)


def feed_forward(sent_rows, w_in, b_in, w_out, b_out, gain_two, shift_two):
    before = jnp.dot(sent_rows, w_in, preferred_element_type=jnp.float32) + b_in
    inner = gelu_exact(before).astype(jnp.bfloat16)
    outer = jnp.dot(inner, w_out, preferred_element_type=jnp.float32) + b_out
    normed, scaled = norm_parts(sent_rows.astype(jnp.float32) + outer)
    result = (normed * gain_two + shift_two).astype(jnp.bfloat16)
    return (result, (before, inner, normed, scaled))


def feed_back(sent_rows, grad_rows, saved, w_in, w_out, gain_two):
    before, inner, normed, scaled = saved
    grad_sum, grad_gain, grad_shift = norm_back(
        grad_rows.astype(jnp.float32), normed, scaled, gain_two
    )
    grad_outer = grad_sum.astype(jnp.bfloat16)
    grad_w_out = row_product(inner, grad_outer)
    grad_inner = back_product(grad_outer, w_out)
    pull = jax.vjp(gelu_exact, before)[1]
    grad_before = pull(grad_inner)[0]
    grad_low = grad_before.astype(jnp.bfloat16)
    grad_w_in = row_product(sent_rows, grad_low)
    grad_sent = (back_product(grad_low, w_in) + grad_sum).astype(jnp.bfloat16)
    grads = (
        grad_w_in,
        jnp.sum(grad_before, axis=0),
        grad_w_out,
        jnp.sum(grad_sum, axis=0),
        grad_gain,
        grad_shift,
    )
    return (grad_sent, grads)


def masked_scores(head_q, head_k, segment):
    scores = jnp.einsum(
        "qhd,khd->hqk", head_q, head_k, preferred_element_type=jnp.float32
    ) * HD ** (-0.5)
    same_doc = segment[:, None] == segment[None, :]
    return jnp.where(same_doc[None], scores, -1e30)


def attend(slot_item):
    queries, key_rows, values, segment = slot_item
    seq_len = queries.shape[0]
    head_q = queries.reshape(seq_len, HEADS, HD)
    head_k = key_rows.reshape(seq_len, HEADS, HD)
    head_v = values.reshape(seq_len, HEADS, HD)
    scores = masked_scores(head_q, head_k, segment)
    row_top = jnp.max(scores, axis=-1, keepdims=True)
    expo = jnp.exp(scores - row_top)
    row_total = jnp.sum(expo, axis=-1, keepdims=True)
    probs = (expo / row_total).astype(jnp.bfloat16)
    mixed = jnp.einsum("hqk,khd->qhd", probs, head_v, preferred_element_type=jnp.float32)
    return (mixed.reshape(seq_len, HEADS * HD).astype(jnp.bfloat16), row_top + jnp.log(row_total))


def attend_back(slot_item):
    queries, key_rows, values, segment, log_total, grad_mixed = slot_item
    seq_len = queries.shape[0]
    head_q = queries.reshape(seq_len, HEADS, HD)
    head_k = key_rows.reshape(seq_len, HEADS, HD)
    head_v = values.reshape(seq_len, HEADS, HD)
    head_g = grad_mixed.reshape(seq_len, HEADS, HD)
    probs = jnp.exp(masked_scores(head_q, head_k, segment) - log_total)
    grad_probs = jnp.einsum("qhd,khd->hqk", head_g, head_v, preferred_element_type=jnp.float32)
    grad_values = jnp.einsum(
        "hqk,qhd->khd", probs.astype(jnp.bfloat16), head_g, preferred_element_type=jnp.float32
    )
    inner_sum = jnp.sum(probs * grad_probs, axis=-1, keepdims=True)
    grad_scores = (probs * (grad_probs - inner_sum)).astype(jnp.bfloat16)
    grad_queries = jnp.einsum(
        "hqk,khd->qhd", grad_scores, head_k, preferred_element_type=jnp.float32
    ) * HD ** (-0.5)
    grad_keys = jnp.einsum(
        "hqk,qhd->khd", grad_scores, head_q, preferred_element_type=jnp.float32
    ) * HD ** (-0.5)
    width_all = HEADS * HD
    return (
        grad_queries.reshape(seq_len, width_all).astype(jnp.bfloat16),
        grad_keys.reshape(seq_len, width_all).astype(jnp.bfloat16),
        grad_values.reshape(seq_len, width_all).astype(jnp.bfloat16),
    )


def on_device(
    inputs,
    cotangent,
    drop_mask,
    doc_len,
    w_query,
    b_query,
    w_key,
    w_value,
    b_value,
    w_attn,
    b_attn,
    gain_one,
    shift_one,
    w_in,
    b_in,
    w_out,
    b_out,
    gain_two,
    shift_two,
):
    tok_rows = inputs[0]
    tok_count, model_width = tok_rows.shape
    slot_count = drop_mask.shape[1]
    doc_count = drop_mask.shape[2]
    seq_len = tok_count // slot_count
    my_index = lax.axis_index("dp")
    wq, bq, wk, wv, bv = (w_query[0], b_query[0], w_key[0], w_value[0], b_value[0])
    wo, bo, gone, sone = (
        w_attn[0],
        b_attn[0],
        gain_one[0].astype(jnp.float32),
        shift_one[0].astype(jnp.float32),
    )
    wi, bi, wu, bu = (w_in[0], b_in[0], w_out[0], b_out[0])
    gtwo, stwo = (gain_two[0].astype(jnp.float32), shift_two[0].astype(jnp.float32))
    ends = jnp.cumsum(doc_len[0], axis=-1)
    places = jnp.arange(seq_len, dtype=jnp.int32)
    segment = jnp.sum((places[None, :, None] >= ends[:, None, :]).astype(jnp.int32), axis=-1)
    segment = jnp.where(my_index % 2 == 0, jnp.zeros_like(segment), segment)
    chosen = segment[:, :, None] == jnp.arange(doc_count, dtype=jnp.int32)[None, None, :]
    dropped = jnp.sum(jnp.where(chosen, drop_mask[0][:, None, :], 0), axis=-1)
    keep = (dropped == 0).reshape(tok_count)
    queries = (jnp.dot(tok_rows, wq, preferred_element_type=jnp.float32) + bq).astype(jnp.bfloat16)
    key_rows = jnp.dot(tok_rows, wk, preferred_element_type=jnp.float32).astype(jnp.bfloat16)
    values = (jnp.dot(tok_rows, wv, preferred_element_type=jnp.float32) + bv).astype(jnp.bfloat16)
    slot_shape = (slot_count, seq_len, model_width)
    mixed, log_total = lax.map(
        attend,
        (
            queries.reshape(slot_shape),
            key_rows.reshape(slot_shape),
            values.reshape(slot_shape),
            segment,
        ),
    )
    mixed = mixed.reshape(tok_count, model_width)
    attended = jnp.dot(mixed, wo, preferred_element_type=jnp.float32) + bo
    normed_one, scaled_one = norm_parts(tok_rows.astype(jnp.float32) + attended)
    sent = (normed_one * gone + sone).astype(jnp.bfloat16)
    final, ffn_saved = feed_forward(sent, wi, bi, wu, bu, gtwo, stwo)
    layer_output = jnp.where(keep[:, None], final, tok_rows)
    out = shifted(layer_output[None], "layer", 1)
    grad_out = shifted(cotangent, "layer", -1)[0]
    grad_kept = jnp.where(keep[:, None], grad_out, jnp.zeros_like(grad_out))
    grad_sent, ffn_grads = feed_back(sent, grad_kept, ffn_saved, wi, wu, gtwo)
    grad_h1, grad_gain_one, grad_shift_one = norm_back(
        grad_sent.astype(jnp.float32), normed_one, scaled_one, gone
    )
    grad_attn = grad_h1.astype(jnp.bfloat16)
    grad_w_attn = row_product(mixed, grad_attn)
    grad_b_attn = jnp.sum(grad_h1, axis=0)
    grad_mixed = back_product(grad_attn, wo).astype(jnp.bfloat16)
    grad_q, grad_k, grad_v = lax.map(
        attend_back,
        (
            queries.reshape(slot_shape),
            key_rows.reshape(slot_shape),
            values.reshape(slot_shape),
            segment,
            log_total,
            grad_mixed.reshape(slot_shape),
        ),
    )
    grad_q = grad_q.reshape(tok_count, model_width)
    grad_k = grad_k.reshape(tok_count, model_width)
    grad_v = grad_v.reshape(tok_count, model_width)
    grad_rows = (
        back_product(grad_q, wq) + back_product(grad_k, wk) + back_product(grad_v, wv) + grad_h1
    )
    grad_inputs = jnp.where(keep[:, None], grad_rows, grad_out.astype(jnp.float32)).astype(
        jnp.bfloat16
    )
    grad_w_query = row_product(tok_rows, grad_q)
    grad_w_key = row_product(tok_rows, grad_k)
    grad_w_value = row_product(tok_rows, grad_v)
    grad_b_query = jnp.sum(grad_q.astype(jnp.float32), axis=0)
    grad_b_value = jnp.sum(grad_v.astype(jnp.float32), axis=0)
    summed = (
        lax.psum(grad_w_query.astype(jnp.bfloat16), "dp").astype(jnp.float32),
        lax.psum(grad_b_query.astype(jnp.bfloat16), "dp").astype(jnp.float32),
        lax.psum(grad_w_key.astype(jnp.bfloat16), "dp").astype(jnp.float32),
        lax.psum(grad_w_value.astype(jnp.bfloat16), "dp").astype(jnp.float32),
        lax.psum(grad_b_value.astype(jnp.bfloat16), "dp").astype(jnp.float32),
        lax.psum(grad_w_attn.astype(jnp.bfloat16), "dp").astype(jnp.float32),
        lax.psum(grad_b_attn.astype(jnp.bfloat16), "dp").astype(jnp.float32),
        lax.psum(grad_gain_one.astype(jnp.bfloat16), "dp").astype(jnp.float32),
        lax.psum(grad_shift_one.astype(jnp.bfloat16), "dp").astype(jnp.float32),
        lax.psum(ffn_grads[0].astype(jnp.bfloat16), "dp").astype(jnp.float32),
        lax.psum(ffn_grads[1].astype(jnp.bfloat16), "dp").astype(jnp.float32),
        lax.psum(ffn_grads[2].astype(jnp.bfloat16), "dp").astype(jnp.float32),
        lax.psum(ffn_grads[3].astype(jnp.bfloat16), "dp").astype(jnp.float32),
        lax.psum(ffn_grads[4].astype(jnp.bfloat16), "dp").astype(jnp.float32),
        lax.psum(ffn_grads[5].astype(jnp.bfloat16), "dp").astype(jnp.float32),
    )
    return (
        out,
        grad_inputs[None],
        summed[0][None],
        summed[1][None],
        summed[2][None],
        summed[3][None],
        summed[4][None],
        summed[5][None],
        summed[6][None],
        summed[7][None],
        summed[8][None],
        summed[9][None],
        summed[10][None],
        summed[11][None],
        summed[12][None],
        summed[13][None],
        summed[14][None],
    )


def solution(mesh):
    in_specs = (
        P("layer", "dp", None),
        P("layer", "dp", None),
        P("layer", "dp", None),
        P("layer", "dp", None),
        P("layer", None, None),
        P("layer", None),
        P("layer", None, None),
        P("layer", None, None),
        P("layer", None),
        P("layer", None, None),
        P("layer", None),
        P("layer", None),
        P("layer", None),
        P("layer", None, None),
        P("layer", None),
        P("layer", None, None),
        P("layer", None),
        P("layer", None),
        P("layer", None),
    )
    out_specs = (
        P("layer", "dp", None),
        P("layer", "dp", None),
        P("layer", None, None),
        P("layer", None),
        P("layer", None, None),
        P("layer", None, None),
        P("layer", None),
        P("layer", None, None),
        P("layer", None),
        P("layer", None),
        P("layer", None),
        P("layer", None, None),
        P("layer", None),
        P("layer", None, None),
        P("layer", None),
        P("layer", None),
        P("layer", None),
    )
    return jax.shard_map(
        on_device, mesh=mesh, in_specs=in_specs, out_specs=out_specs, check_vma=False
    )
```

```python
import functools

import jax
import jax.numpy as jnp
from jax import lax
from jax.experimental import pallas as pl
from jax.experimental.pallas import tpu as pltpu
from jax.sharding import PartitionSpec as P

HEADS = 12
HD = 64


eps_norm = 1e-05


def shifted(block, axis, distance):
    devices = range(lax.axis_size(axis))
    route = [((i - distance) % len(devices), i) for i in devices]
    return lax.ppermute(block, axis, route)


def crossed(block, bit):
    route = [(i, i ^ (1 << bit)) for i in range(lax.axis_size("dp"))]
    return lax.ppermute(block, "dp", route)


def dp_bits():
    return list(range((lax.axis_size("dp") - 1).bit_length()))


class GroupSum:
    def __init__(self, block):
        bits = dp_bits()
        half = block.shape[0] // 2
        self.blocks = [block[:half], block[half:]]
        orders = (bits, bits[:1] + bits[:0:-1])
        self.steps = [(True, pair) for pair in zip(*orders)]
        self.steps += [(False, pair) for pair in list(zip(*orders))[::-1]]
        self.pieces = ()

    def side(self, bit):
        return (lax.axis_index("dp") >> bit) & 1

    def start(self):
        if not self.steps:
            return []
        adding, pair = self.steps[0]
        sent = self.blocks
        if adding:
            sent = [
                lax.dynamic_slice_in_dim(
                    block, (1 - self.side(bit)) * (block.shape[0] // 2), block.shape[0] // 2, 0
                )
                for block, bit in zip(self.blocks, pair)
            ]
        return [crossed(block, bit) for block, bit in zip(sent, pair)]

    def finish(self, received):
        if not self.steps:
            return
        adding, pair = self.steps.pop(0)
        if not self.steps:
            self.pieces = (self.blocks[0], received[0], self.blocks[1], received[1])
            return
        for idx, bit in enumerate(pair):
            block, got = (self.blocks[idx], received[idx])
            if adding:
                half = block.shape[0] // 2
                own = lax.dynamic_slice_in_dim(block, self.side(bit) * half, half, 0)
                total = own.astype(jnp.float32) + got.astype(jnp.float32)
                self.blocks[idx] = total.astype(jnp.bfloat16)
            else:
                self.blocks[idx] = jnp.where(
                    self.side(bit) == 1,
                    jnp.concatenate([got, block]),
                    jnp.concatenate([block, got]),
                )

    def placed(self, out_count=1):
        while self.steps:
            self.finish(self.start())
        return placed(self.pieces, self.side(0), out_count)


def beside(value, *sums):
    received = [one.start() for one in sums]
    value, received = lax.optimization_barrier((value, received))
    for one, got in zip(sums, received):
        one.finish(got)
    return value


def place_kernel(side_ref, own_a, got_a, own_b, got_b, *outs):
    quarter = pl.program_id(0)
    width = outs[0].shape[-1]
    is_own = quarter % 2 == side_ref[0]

    def put(source):
        for idx, out_ref in enumerate(outs):
            out_ref[0] = source[:, idx * width : (idx + 1) * width].astype(jnp.float32)

    for stream, (own, got) in enumerate(((own_a, got_a), (own_b, got_b))):
        pl.when((quarter // 2 == stream) & is_own)(functools.partial(put, own))
        pl.when((quarter // 2 == stream) & jnp.logical_not(is_own))(functools.partial(put, got))


def placed(pieces, side, out_count):
    rows, width = pieces[0].shape
    blocks = max(1, rows * width * 4 // 2**21)
    tall = rows // blocks

    def source_map(stream, wants_own, quarter, idx, side_ref):
        is_own = (quarter % 2 == side_ref[0]).astype(jnp.int32)
        active = (quarter // 2 == stream) & (is_own == wants_own)
        return (jnp.where(active, idx, 0), 0)

    return pl.pallas_call(
        place_kernel,
        grid_spec=pltpu.PrefetchScalarGridSpec(
            num_scalar_prefetch=1,
            grid=(4, blocks),
            in_specs=[
                pl.BlockSpec((tall, width), functools.partial(source_map, stream, own))
                for stream in (0, 1)
                for own in (1, 0)
            ],
            out_specs=[
                pl.BlockSpec(
                    (1, tall, width // out_count), lambda q, i, side_ref: (0, q * blocks + i, 0)
                )
                for _ in range(out_count)
            ],
        ),
        out_shape=[
            jax.ShapeDtypeStruct((1, rows * 4, width // out_count), jnp.float32)
            for _ in range(out_count)
        ],
        cost_estimate=pl.CostEstimate(
            flops=rows * width * 4, bytes_accessed=rows * width * 24, transcendentals=0
        ),
    )(side.reshape(1), *pieces)


def group_sum_rows(vectors):
    for bit in dp_bits():
        vectors = vectors + crossed(vectors, bit)
    return vectors


def norm_parts(values):
    center = jnp.mean(values, axis=-1, keepdims=True)
    centered = values - center
    spread = jnp.mean(centered * centered, axis=-1, keepdims=True)
    scaled = lax.rsqrt(spread + eps_norm)
    return (centered * scaled, scaled)


def norm_back(grad_out, normed, scaled, gain):
    grad_norm = grad_out * gain
    first_mean = jnp.mean(grad_norm, axis=-1, keepdims=True)
    second_mean = jnp.mean(grad_norm * normed, axis=-1, keepdims=True)
    grad_in = scaled * (grad_norm - first_mean - normed * second_mean)
    return (grad_in, jnp.sum(grad_out * normed, axis=0), jnp.sum(grad_out, axis=0))


def row_product(left, right):
    return jnp.einsum("nd,nf->df", left, right, preferred_element_type=jnp.float32)


def back_product(left, right):
    return jnp.einsum("nf,df->nd", left, right, preferred_element_type=jnp.float32)


def gelu_exact(values):
    return jax.nn.gelu(values, approximate=False)


def feed_forward(sent_rows, w_in, b_in, w_out, b_out, gain_two, shift_two):
    before = jnp.dot(sent_rows, w_in, preferred_element_type=jnp.float32) + b_in
    inner = gelu_exact(before).astype(jnp.bfloat16)
    outer = jnp.dot(inner, w_out, preferred_element_type=jnp.float32) + b_out
    normed, scaled = norm_parts(sent_rows.astype(jnp.float32) + outer)
    result = (normed * gain_two + shift_two).astype(jnp.bfloat16)
    return (result, (before, inner, normed, scaled))


def head_rows(block, head):
    lane = lax.broadcasted_iota(jnp.int32, block.shape, 1)
    return jnp.where(lane // HD == head, block, jnp.zeros_like(block))


def turned(block):
    return block.astype(jnp.float32).T


def across(left, right):
    return lax.dot_general(
        left, right, (((1,), (1,)), ((), ())), preferred_element_type=jnp.float32
    )


def attend_kernel(q_ref, k_ref, v_ref, seg_row_ref, seg_col_ref, mixed_ref, log_ref):
    queries, key_rows = q_ref[...], k_ref[...]
    values_t = turned(v_ref[...]).astype(jnp.bfloat16)
    same_doc = seg_col_ref[0] == seg_row_ref[0]
    parts = []
    for head in range(2):
        own = head_rows(queries, head) * jnp.asarray(HD ** (-0.5), jnp.bfloat16)
        scores = jnp.where(same_doc, across(key_rows, own), -1e30)
        top = jnp.max(scores, axis=0, keepdims=True)
        expo = jnp.exp(scores - top)
        total = jnp.sum(expo, axis=0, keepdims=True)
        mixed = jnp.dot(
            values_t[head * HD : (head + 1) * HD],
            expo.astype(jnp.bfloat16),
            preferred_element_type=jnp.float32,
        )
        parts.append(mixed / total)
        log_ref[0, 0, head : head + 1] = top + jnp.log(total)
    mixed_ref[...] = jnp.concatenate(parts, axis=0).T.astype(jnp.bfloat16)


def attend_back_kernel(q_ref, k_ref, v_ref, g_ref, seg_row_ref, seg_col_ref, log_ref, *rest):
    dq_ref, dk_ref, dv_ref = rest[-3:]

    queries, key_rows, values, grads = q_ref[...], k_ref[...], v_ref[...], g_ref[...]
    scale = HD ** (-0.5)
    keys_t = turned(key_rows).astype(jnp.bfloat16)
    same_doc = seg_col_ref[0] == seg_row_ref[0]
    grad_k = jnp.zeros(key_rows.shape, jnp.float32)
    grad_v = jnp.zeros(key_rows.shape, jnp.float32)
    parts = []
    for head in range(2):
        own = head_rows(queries, head) * jnp.asarray(scale, jnp.bfloat16)
        own_grad = head_rows(grads, head)
        scores = jnp.where(same_doc, across(key_rows, own), -1e30)
        probs = jnp.exp(scores - log_ref[0, 0, head : head + 1])
        grad_probs = across(values, own_grad)
        grad_v = grad_v + jnp.dot(
            probs.astype(jnp.bfloat16), own_grad, preferred_element_type=jnp.float32
        )
        inner_sum = jnp.sum(probs * grad_probs, axis=0, keepdims=True)
        grad_scores = (probs * (grad_probs - inner_sum)).astype(jnp.bfloat16)
        grad_k = grad_k + jnp.dot(grad_scores, own, preferred_element_type=jnp.float32)
        parts.append(
            jnp.dot(
                keys_t[head * HD : (head + 1) * HD],
                grad_scores,
                preferred_element_type=jnp.float32,
            )
        )
    dq_ref[...] = (jnp.concatenate(parts, axis=0).T * scale).astype(jnp.bfloat16)
    dk_ref[...] = grad_k.astype(jnp.bfloat16)
    dv_ref[...] = grad_v.astype(jnp.bfloat16)


def attention_specs(first_slot, seq_len, pairs):
    def part(which):
        return pl.BlockSpec((seq_len, 2 * HD), lambda s, p: (s + first_slot, which * pairs + p))

    seg_specs = [
        pl.BlockSpec((1, 1, seq_len), lambda s, p: (s + first_slot, 0, 0)),
        pl.BlockSpec((1, seq_len, 1), lambda s, p: (s + first_slot, 0, 0)),
    ]
    log_spec = pl.BlockSpec((1, 1, 2, seq_len), lambda s, p: (s + first_slot, p, 0, 0))
    return (part, seg_specs, log_spec)


def attend(qkv, segment):
    slot_count, seq_len = segment.shape
    width = qkv.shape[1] // 3
    pairs = width // (2 * HD)
    part, seg_specs, log_spec = attention_specs(0, seq_len, pairs)
    work = slot_count * pairs * 2 * seq_len * seq_len
    return pl.pallas_call(
        attend_kernel,
        grid=(slot_count, pairs),
        in_specs=[part(0), part(1), part(2)] + seg_specs,
        out_specs=[part(0), log_spec],
        out_shape=[
            jax.ShapeDtypeStruct((qkv.shape[0], width), jnp.bfloat16),
            jax.ShapeDtypeStruct((slot_count, pairs, 2, seq_len), jnp.float32),
        ],
        cost_estimate=pl.CostEstimate(
            flops=work * 8 * HD, bytes_accessed=qkv.size * 3, transcendentals=work
        ),
    )(qkv, qkv, qkv, segment[:, None, :], segment[:, :, None])


def attend_back(qkv, grad_mixed, segment, log_total, first_slot, end_slot, earlier=()):
    seq_len = segment.shape[1]
    width = qkv.shape[1] // 3
    pairs = width // (2 * HD)
    part, seg_specs, log_spec = attention_specs(first_slot, seq_len, pairs)
    work = (end_slot - first_slot) * pairs * 2 * seq_len * seq_len
    return pl.pallas_call(
        attend_back_kernel,
        grid=(end_slot - first_slot, pairs),
        in_specs=[part(0), part(1), part(2), part(0)]
        + seg_specs
        + [log_spec]
        + [pl.BlockSpec(memory_space=pl.ANY)] * len(earlier),
        out_specs=[part(0), part(0), part(0)],
        out_shape=[jax.ShapeDtypeStruct((qkv.shape[0], width), jnp.bfloat16)] * 3,
        input_output_aliases={7 + idx: idx for idx in range(len(earlier))},
        cost_estimate=pl.CostEstimate(
            flops=work * 20 * HD, bytes_accessed=qkv.size * 2, transcendentals=work
        ),
    )(qkv, qkv, qkv, grad_mixed, segment[:, None, :], segment[:, :, None], log_total, *earlier)


def on_device(
    inputs,
    cotangent,
    drop_mask,
    doc_len,
    w_query,
    b_query,
    w_key,
    w_value,
    b_value,
    w_attn,
    b_attn,
    gain_one,
    shift_one,
    w_in,
    b_in,
    w_out,
    b_out,
    gain_two,
    shift_two,
):
    tok_rows = inputs[0]
    tok_count, model_width = tok_rows.shape
    slot_count = drop_mask.shape[1]
    doc_count = drop_mask.shape[2]
    seq_len = tok_count // slot_count
    my_index = lax.axis_index("dp")
    wq, bq, wk, wv, bv = (w_query[0], b_query[0], w_key[0], w_value[0], b_value[0])
    wo, bo, gone, sone = (
        w_attn[0],
        b_attn[0],
        gain_one[0].astype(jnp.float32),
        shift_one[0].astype(jnp.float32),
    )
    wi, bi, wu, bu = (w_in[0], b_in[0], w_out[0], b_out[0])
    gtwo, stwo = (gain_two[0].astype(jnp.float32), shift_two[0].astype(jnp.float32))
    ends = jnp.cumsum(doc_len[0], axis=-1)
    places = jnp.arange(seq_len, dtype=jnp.int32)
    segment = jnp.sum((places[None, :, None] >= ends[:, None, :]).astype(jnp.int32), axis=-1)
    segment = jnp.where(my_index % 2 == 0, jnp.zeros_like(segment), segment)
    chosen = segment[:, :, None] == jnp.arange(doc_count, dtype=jnp.int32)[None, None, :]
    dropped = jnp.sum(jnp.where(chosen, drop_mask[0][:, None, :], 0), axis=-1)
    keep = (dropped == 0).reshape(tok_count)
    w_three = jnp.concatenate([wq, wk, wv], axis=1)
    b_three = jnp.concatenate([bq, jnp.zeros_like(bq), bv])
    qkv = (jnp.dot(tok_rows, w_three, preferred_element_type=jnp.float32) + b_three).astype(
        jnp.bfloat16
    )
    mixed, log_total = attend(qkv, segment)
    attended = jnp.dot(mixed, wo, preferred_element_type=jnp.float32) + bo
    normed_one, scaled_one = norm_parts(tok_rows.astype(jnp.float32) + attended)
    sent = (normed_one * gone + sone).astype(jnp.bfloat16)
    final, ffn_saved = feed_forward(sent, wi, bi, wu, bu, gtwo, stwo)
    layer_output = jnp.where(keep[:, None], final, tok_rows)
    out = shifted(layer_output[None], "layer", 1)
    grad_out = shifted(cotangent, "layer", -1)[0]
    grad_kept = jnp.where(keep[:, None], grad_out, jnp.zeros_like(grad_out))
    before, inner, normed_two, scaled_two = ffn_saved
    grad_sum, grad_gain_two, grad_shift_two = norm_back(
        grad_kept.astype(jnp.float32), normed_two, scaled_two, gtwo
    )
    grad_outer = grad_sum.astype(jnp.bfloat16)
    low_w_out, grad_outer = lax.optimization_barrier(
        (row_product(inner, grad_outer).astype(jnp.bfloat16), grad_outer)
    )
    sum_out = GroupSum(low_w_out)
    grad_inner = back_product(grad_outer, wu)
    grad_before = jax.vjp(gelu_exact, before)[1](grad_inner)[0]
    grad_b_in = jnp.sum(grad_before, axis=0)
    grad_low, grad_b_in = beside((grad_before.astype(jnp.bfloat16), grad_b_in), sum_out)
    low_w_in, grad_low = beside(
        (row_product(sent, grad_low).astype(jnp.bfloat16), grad_low), sum_out
    )
    sum_in = GroupSum(low_w_in)
    grad_sent = (back_product(grad_low, wi) + grad_sum).astype(jnp.bfloat16)
    grad_h1, grad_gain_one, grad_shift_one = norm_back(
        grad_sent.astype(jnp.float32), normed_one, scaled_one, gone
    )
    grad_attn = grad_h1.astype(jnp.bfloat16)
    grad_w_attn = row_product(mixed, grad_attn).astype(jnp.bfloat16)
    grad_b_attn = jnp.sum(grad_h1, axis=0)
    grad_mixed = back_product(grad_attn, wo).astype(jnp.bfloat16)
    grad_mixed, grad_w_attn, out = beside((grad_mixed, grad_w_attn, out), sum_out, sum_in)
    middle = slot_count // 2
    attention = (qkv, grad_mixed, segment, log_total)
    grads_qkv = beside(attend_back(*attention, 0, middle), sum_out, sum_in)
    grads_qkv = beside(
        attend_back(*attention, middle, slot_count, tuple(grads_qkv)), sum_out, sum_in
    )
    grad_q, grad_k, grad_v = grads_qkv
    low_attention = jnp.concatenate(
        [row_product(tok_rows, grad).astype(jnp.bfloat16) for grad in grads_qkv] + [grad_w_attn],
        axis=1,
    )
    low_attention, grad_q, grad_k, grad_v = beside(
        (low_attention, grad_q, grad_k, grad_v), sum_out, sum_in
    )
    sum_attention = GroupSum(low_attention)
    grad_rows = (
        back_product(grad_q, wq) + back_product(grad_k, wk) + back_product(grad_v, wv) + grad_h1
    )
    grad_inputs = jnp.where(keep[:, None], grad_rows, grad_out.astype(jnp.float32)).astype(
        jnp.bfloat16
    )
    grad_b_query = jnp.sum(grad_q.astype(jnp.float32), axis=0)
    grad_b_value = jnp.sum(grad_v.astype(jnp.float32), axis=0)
    grad_inputs, grad_b_query, grad_b_value = beside(
        (grad_inputs, grad_b_query, grad_b_value), sum_in, sum_attention
    )
    (sum_w_out,) = beside(sum_out.placed(), sum_in, sum_attention)
    (sum_w_in,) = beside(sum_in.placed(), sum_attention)
    attention_sums = sum_attention.placed(4)
    rows = group_sum_rows(
        jnp.concatenate(
            [
                vector.reshape(-1, model_width)
                for vector in (
                    grad_b_query,
                    grad_b_value,
                    grad_b_attn,
                    grad_gain_one,
                    grad_shift_one,
                    jnp.sum(grad_sum, axis=0),
                    grad_gain_two,
                    grad_shift_two,
                    grad_b_in,
                )
            ]
        )
    )
    return (
        out,
        grad_inputs[None],
        attention_sums[0],
        rows[0][None],
        attention_sums[1],
        attention_sums[2],
        rows[1][None],
        attention_sums[3],
        rows[2][None],
        rows[3][None],
        rows[4][None],
        sum_w_in,
        rows[8:].reshape(1, -1),
        sum_w_out,
        rows[5][None],
        rows[6][None],
        rows[7][None],
    )


def solution(mesh):
    in_specs = (
        P("layer", "dp", None),
        P("layer", "dp", None),
        P("layer", "dp", None),
        P("layer", "dp", None),
        P("layer", None, None),
        P("layer", None),
        P("layer", None, None),
        P("layer", None, None),
        P("layer", None),
        P("layer", None, None),
        P("layer", None),
        P("layer", None),
        P("layer", None),
        P("layer", None, None),
        P("layer", None),
        P("layer", None, None),
        P("layer", None),
        P("layer", None),
        P("layer", None),
    )
    out_specs = (
        P("layer", "dp", None),
        P("layer", "dp", None),
        P("layer", None, None),
        P("layer", None),
        P("layer", None, None),
        P("layer", None, None),
        P("layer", None),
        P("layer", None, None),
        P("layer", None),
        P("layer", None),
        P("layer", None),
        P("layer", None, None),
        P("layer", None),
        P("layer", None, None),
        P("layer", None),
        P("layer", None),
        P("layer", None),
    )
    return jax.shard_map(
        on_device, mesh=mesh, in_specs=in_specs, out_specs=out_specs, check_vma=False
    )
```

```python
import functools

import jax
import jax.numpy as jnp
from jax import lax
from jax.experimental import pallas as pl
from jax.experimental.pallas import tpu as pltpu
from jax.sharding import PartitionSpec as P

HEADS = 12
HD = 64


eps_norm = 1e-05


def shifted(block, axis, distance):
    devices = range(lax.axis_size(axis))
    route = [((i - distance) % len(devices), i) for i in devices]
    return lax.ppermute(block, axis, route)


def crossed(block, bit):
    route = [(i, i ^ (1 << bit)) for i in range(lax.axis_size("dp"))]
    return lax.ppermute(block, "dp", route)


def dp_bits():
    return list(range((lax.axis_size("dp") - 1).bit_length()))


class GroupSum:
    def __init__(self, block):
        bits = dp_bits()
        half = block.shape[0] // 2
        self.blocks = [block[:half], block[half:]]
        orders = (bits, bits[:1] + bits[:0:-1])
        self.steps = [(True, pair) for pair in zip(*orders)]
        self.steps += [(False, pair) for pair in list(zip(*orders))[::-1]]
        self.pieces = ()

    def side(self, bit):
        return (lax.axis_index("dp") >> bit) & 1

    def start(self):
        if not self.steps:
            return []
        adding, pair = self.steps[0]
        sent = self.blocks
        if adding:
            sent = [
                lax.dynamic_slice_in_dim(
                    block, (1 - self.side(bit)) * (block.shape[0] // 2), block.shape[0] // 2, 0
                )
                for block, bit in zip(self.blocks, pair)
            ]
        return [crossed(block, bit) for block, bit in zip(sent, pair)]

    def finish(self, received):
        if not self.steps:
            return
        adding, pair = self.steps.pop(0)
        if not self.steps:
            self.pieces = (self.blocks[0], received[0], self.blocks[1], received[1])
            return
        for idx, bit in enumerate(pair):
            block, got = (self.blocks[idx], received[idx])
            if adding:
                half = block.shape[0] // 2
                own = lax.dynamic_slice_in_dim(block, self.side(bit) * half, half, 0)
                total = own.astype(jnp.float32) + got.astype(jnp.float32)
                self.blocks[idx] = total.astype(jnp.bfloat16)
            else:
                self.blocks[idx] = jnp.where(
                    self.side(bit) == 1,
                    jnp.concatenate([got, block]),
                    jnp.concatenate([block, got]),
                )

    def placed(self, out_count=1):
        while self.steps:
            self.finish(self.start())
        return placed(self.pieces, self.side(0), out_count)


def beside(value, *sums):
    received = [one.start() for one in sums]
    value, received = lax.optimization_barrier((value, received))
    for one, got in zip(sums, received):
        one.finish(got)
    return value


def place_kernel(side_ref, own_a, got_a, own_b, got_b, *outs):
    quarter = pl.program_id(0)
    width = outs[0].shape[-1]
    is_own = quarter % 2 == side_ref[0]

    def put(source):
        for idx, out_ref in enumerate(outs):
            out_ref[0] = source[:, idx * width : (idx + 1) * width].astype(jnp.float32)

    for stream, (own, got) in enumerate(((own_a, got_a), (own_b, got_b))):
        pl.when((quarter // 2 == stream) & is_own)(functools.partial(put, own))
        pl.when((quarter // 2 == stream) & jnp.logical_not(is_own))(functools.partial(put, got))


def placed(pieces, side, out_count):
    rows, width = pieces[0].shape
    blocks = max(1, rows * width * 4 // 2**21)
    tall = rows // blocks

    def source_map(stream, wants_own, quarter, idx, side_ref):
        is_own = (quarter % 2 == side_ref[0]).astype(jnp.int32)
        active = (quarter // 2 == stream) & (is_own == wants_own)
        return (jnp.where(active, idx, 0), 0)

    return pl.pallas_call(
        place_kernel,
        grid_spec=pltpu.PrefetchScalarGridSpec(
            num_scalar_prefetch=1,
            grid=(4, blocks),
            in_specs=[
                pl.BlockSpec((tall, width), functools.partial(source_map, stream, own))
                for stream in (0, 1)
                for own in (1, 0)
            ],
            out_specs=[
                pl.BlockSpec(
                    (1, tall, width // out_count), lambda q, i, side_ref: (0, q * blocks + i, 0)
                )
                for _ in range(out_count)
            ],
        ),
        out_shape=[
            jax.ShapeDtypeStruct((1, rows * 4, width // out_count), jnp.float32)
            for _ in range(out_count)
        ],
        cost_estimate=pl.CostEstimate(
            flops=rows * width * 4, bytes_accessed=rows * width * 24, transcendentals=0
        ),
    )(side.reshape(1), *pieces)


def widen_kernel(low_ref, out_ref):
    out_ref[0] = low_ref[...].astype(jnp.float32)


def widened(low):
    rows, width = low.shape
    steps = max(1, rows * width * 4 // 2**20 // 2)
    while rows % (steps * 16):
        steps -= 1
    return pl.pallas_call(
        widen_kernel,
        grid=(steps,),
        in_specs=[pl.BlockSpec((rows // steps, width), lambda i: (i, 0))],
        out_specs=pl.BlockSpec((1, rows // steps, width), lambda i: (0, i, 0)),
        out_shape=jax.ShapeDtypeStruct((1, rows, width), jnp.float32),
        cost_estimate=pl.CostEstimate(
            flops=rows * width, bytes_accessed=rows * width * 6, transcendentals=0
        ),
    )(low)


class RowSum:
    def __init__(self, rows):
        self.rows = rows
        self.bits = dp_bits()

    def start(self):
        return [crossed(self.rows, self.bits[0])] if self.bits else []

    def finish(self, received):
        if self.bits:
            self.bits.pop(0)
            self.rows = self.rows + received[0]

    def total(self):
        while self.bits:
            self.finish(self.start())
        return self.rows


def norm_parts(values):
    center = jnp.mean(values, axis=-1, keepdims=True)
    centered = values - center
    spread = jnp.mean(centered * centered, axis=-1, keepdims=True)
    scaled = lax.rsqrt(spread + eps_norm)
    return (centered * scaled, scaled)


def norm_back(grad_out, normed, scaled, gain):
    grad_norm = grad_out * gain
    first_mean = jnp.mean(grad_norm, axis=-1, keepdims=True)
    second_mean = jnp.mean(grad_norm * normed, axis=-1, keepdims=True)
    grad_in = scaled * (grad_norm - first_mean - normed * second_mean)
    return (grad_in, jnp.sum(grad_out * normed, axis=0), jnp.sum(grad_out, axis=0))


def row_product(left, right):
    return jnp.einsum("nd,nf->df", left, right, preferred_element_type=jnp.float32)


def back_product(left, right):
    return jnp.einsum("nf,df->nd", left, right, preferred_element_type=jnp.float32)


def gelu_parts(values):
    cumulative = 0.5 + 0.5 * lax.erf(values * 0.5**0.5)
    density = jnp.exp(-0.5 * values * values) * (0.5 / jnp.pi) ** 0.5
    return (values * cumulative, cumulative + values * density)


def feed_kernel(
    sent_ref,
    w_in_ref,
    b_in_ref,
    w_out_ref,
    rows_ref,
    grad_ref,
    keep_ref,
    tok_ref,
    inner_ref,
    slope_ref,
    out_ref,
    low_ref,
    grad_sum_ref,
    vectors_ref,
):
    sent = sent_ref[...]
    width_in = w_in_ref.shape[1]
    chunk = 512 if width_in % 512 == 0 else width_in
    outer = jnp.zeros(sent.shape, jnp.float32)
    for start in range(0, width_in, chunk):
        cols = slice(start, start + chunk)
        before = (
            jnp.dot(sent, w_in_ref[:, cols], preferred_element_type=jnp.float32)
            + b_in_ref[:, cols]
        )
        inner, slope = gelu_parts(before)
        inner = inner.astype(jnp.bfloat16)
        inner_ref[:, cols] = inner
        slope_ref[:, cols] = slope.astype(jnp.bfloat16)
        outer = outer + jnp.dot(inner, w_out_ref[cols, :], preferred_element_type=jnp.float32)
    kept = keep_ref[...] > 0
    b_out, gain, shift = rows_ref[0:1], rows_ref[1:2], rows_ref[2:3]
    normed, scaled = norm_parts(sent.astype(jnp.float32) + (outer + b_out))
    final = (normed * gain + shift).astype(jnp.bfloat16)
    out_ref[...] = jnp.where(kept, final, tok_ref[...])
    grad_rows = jnp.where(kept, grad_ref[...].astype(jnp.float32), 0.0)
    grad_sum, grad_gain, grad_shift = norm_back(grad_rows, normed, scaled, gain)
    grad_sum_ref[...] = grad_sum
    low_ref[...] = grad_sum.astype(jnp.bfloat16)

    @pl.when(pl.program_id(0) == 0)
    def _():
        vectors_ref[...] = jnp.zeros_like(vectors_ref)

    vectors_ref[0:1] += jnp.sum(grad_sum, axis=0, keepdims=True)
    vectors_ref[1:2] += grad_gain[None]
    vectors_ref[2:3] += grad_shift[None]


def feed_forward(sent, w_in, b_in, w_out, rows, grad_out, keep, tok_rows):
    count, width = sent.shape
    wide = w_in.shape[1]
    tall = 256 if count % 256 == 0 else count

    def whole(array):
        return pl.BlockSpec(array.shape, lambda i: (0, 0), pipeline_mode=pl.Buffered(1))

    narrow_spec = pl.BlockSpec((tall, width), lambda i: (i, 0))
    wide_spec = pl.BlockSpec((tall, wide), lambda i: (i, 0))
    return pl.pallas_call(
        feed_kernel,
        grid=(count // tall,),
        in_specs=[
            narrow_spec,
            whole(w_in),
            whole(b_in),
            whole(w_out),
            whole(rows),
            narrow_spec,
            pl.BlockSpec((tall, 1), lambda i: (i, 0)),
            narrow_spec,
        ],
        out_specs=[
            wide_spec,
            wide_spec,
            narrow_spec,
            narrow_spec,
            narrow_spec,
            pl.BlockSpec((8, width), lambda i: (0, 0)),
        ],
        out_shape=[
            jax.ShapeDtypeStruct((count, wide), jnp.bfloat16),
            jax.ShapeDtypeStruct((count, wide), jnp.bfloat16),
            jax.ShapeDtypeStruct((count, width), jnp.bfloat16),
            jax.ShapeDtypeStruct((count, width), jnp.bfloat16),
            jax.ShapeDtypeStruct((count, width), jnp.float32),
            jax.ShapeDtypeStruct((8, width), jnp.float32),
        ],
        compiler_params=pltpu.CompilerParams(vmem_limit_bytes=56 * 2**20),
        cost_estimate=pl.CostEstimate(
            flops=count * width * wide * 4,
            bytes_accessed=count * wide * 4 + wide * width * 4,
            transcendentals=count * wide * 2,
        ),
    )(sent, w_in, b_in, w_out, rows, grad_out, keep, tok_rows)


def slope_kernel(low_ref, w_out_ref, slope_ref, grad_ref, sums_ref):
    grad = across(low_ref[...], w_out_ref[...]) * slope_ref[...].astype(jnp.float32)
    grad_ref[...] = grad.astype(jnp.bfloat16)
    sums_ref[...] = jnp.sum(grad, axis=0, keepdims=True)


def slope_back(low, w_out, slope):
    count, width = low.shape
    wide = w_out.shape[0]
    chunk = 512 if wide % 512 == 0 else wide
    return pl.pallas_call(
        slope_kernel,
        grid=(wide // chunk,),
        in_specs=[
            pl.BlockSpec((count, width), lambda i: (0, 0), pipeline_mode=pl.Buffered(1)),
            pl.BlockSpec((chunk, width), lambda i: (i, 0)),
            pl.BlockSpec((count, chunk), lambda i: (0, i)),
        ],
        out_specs=[
            pl.BlockSpec((count, chunk), lambda i: (0, i)),
            pl.BlockSpec((1, chunk), lambda i: (0, i)),
        ],
        out_shape=[
            jax.ShapeDtypeStruct((count, wide), jnp.bfloat16),
            jax.ShapeDtypeStruct((1, wide), jnp.float32),
        ],
        cost_estimate=pl.CostEstimate(
            flops=count * width * wide * 2, bytes_accessed=count * wide * 4, transcendentals=0
        ),
    )(low, w_out, slope)


def head_rows(block, head):
    lane = lax.broadcasted_iota(jnp.int32, block.shape, 1)
    return jnp.where(lane // HD == head, block, jnp.zeros_like(block))


def turned(block):
    return block.astype(jnp.float32).T


def across(left, right):
    return lax.dot_general(
        left, right, (((1,), (1,)), ((), ())), preferred_element_type=jnp.float32
    )


def attend_kernel(q_ref, k_ref, v_ref, seg_row_ref, seg_col_ref, mixed_ref, log_ref):
    queries, key_rows = q_ref[...], k_ref[...]
    values_t = turned(v_ref[...]).astype(jnp.bfloat16)
    same_doc = seg_col_ref[0] == seg_row_ref[0]
    parts = []
    for head in range(2):
        own = head_rows(queries, head) * jnp.asarray(HD ** (-0.5), jnp.bfloat16)
        scores = jnp.where(same_doc, across(key_rows, own), -1e30)
        top = jnp.max(scores, axis=0, keepdims=True)
        expo = jnp.exp(scores - top)
        total = jnp.sum(expo, axis=0, keepdims=True)
        mixed = jnp.dot(
            values_t[head * HD : (head + 1) * HD],
            expo.astype(jnp.bfloat16),
            preferred_element_type=jnp.float32,
        )
        parts.append(mixed / total)
        log_ref[0, 0, head : head + 1] = top + jnp.log(total)
    mixed_ref[...] = jnp.concatenate(parts, axis=0).T.astype(jnp.bfloat16)


def attend_back_kernel(q_ref, k_ref, v_ref, g_ref, seg_row_ref, seg_col_ref, log_ref, *rest):
    dq_ref, dk_ref, dv_ref = rest[-3:]

    queries, key_rows, values, grads = q_ref[...], k_ref[...], v_ref[...], g_ref[...]
    scale = HD ** (-0.5)
    keys_t = turned(key_rows).astype(jnp.bfloat16)
    same_doc = seg_col_ref[0] == seg_row_ref[0]
    grad_k = jnp.zeros(key_rows.shape, jnp.float32)
    grad_v = jnp.zeros(key_rows.shape, jnp.float32)
    parts = []
    for head in range(2):
        own = head_rows(queries, head) * jnp.asarray(scale, jnp.bfloat16)
        own_grad = head_rows(grads, head)
        scores = jnp.where(same_doc, across(key_rows, own), -1e30)
        probs = jnp.exp(scores - log_ref[0, 0, head : head + 1])
        grad_probs = across(values, own_grad)
        grad_v = grad_v + jnp.dot(
            probs.astype(jnp.bfloat16), own_grad, preferred_element_type=jnp.float32
        )
        inner_sum = jnp.sum(probs * grad_probs, axis=0, keepdims=True)
        grad_scores = (probs * (grad_probs - inner_sum)).astype(jnp.bfloat16)
        grad_k = grad_k + jnp.dot(grad_scores, own, preferred_element_type=jnp.float32)
        parts.append(
            jnp.dot(
                keys_t[head * HD : (head + 1) * HD],
                grad_scores,
                preferred_element_type=jnp.float32,
            )
        )
    dq_ref[...] = (jnp.concatenate(parts, axis=0).T * scale).astype(jnp.bfloat16)
    dk_ref[...] = grad_k.astype(jnp.bfloat16)
    dv_ref[...] = grad_v.astype(jnp.bfloat16)


def attention_specs(first_slot, seq_len, pairs):
    def part(which):
        return pl.BlockSpec((seq_len, 2 * HD), lambda s, p: (s + first_slot, which * pairs + p))

    seg_specs = [
        pl.BlockSpec((1, 1, seq_len), lambda s, p: (s + first_slot, 0, 0)),
        pl.BlockSpec((1, seq_len, 1), lambda s, p: (s + first_slot, 0, 0)),
    ]
    log_spec = pl.BlockSpec((1, 1, 2, seq_len), lambda s, p: (s + first_slot, p, 0, 0))
    return (part, seg_specs, log_spec)


def attend(qkv, segment):
    slot_count, seq_len = segment.shape
    width = qkv.shape[1] // 3
    pairs = width // (2 * HD)
    part, seg_specs, log_spec = attention_specs(0, seq_len, pairs)
    work = slot_count * pairs * 2 * seq_len * seq_len
    return pl.pallas_call(
        attend_kernel,
        grid=(slot_count, pairs),
        in_specs=[part(0), part(1), part(2)] + seg_specs,
        out_specs=[part(0), log_spec],
        out_shape=[
            jax.ShapeDtypeStruct((qkv.shape[0], width), jnp.bfloat16),
            jax.ShapeDtypeStruct((slot_count, pairs, 2, seq_len), jnp.float32),
        ],
        cost_estimate=pl.CostEstimate(
            flops=work * 8 * HD, bytes_accessed=qkv.size * 3, transcendentals=work
        ),
    )(qkv, qkv, qkv, segment[:, None, :], segment[:, :, None])


def attend_back(qkv, grad_mixed, segment, log_total, first_slot, end_slot, earlier=()):
    seq_len = segment.shape[1]
    width = qkv.shape[1] // 3
    pairs = width // (2 * HD)
    part, seg_specs, log_spec = attention_specs(first_slot, seq_len, pairs)
    work = (end_slot - first_slot) * pairs * 2 * seq_len * seq_len
    return pl.pallas_call(
        attend_back_kernel,
        grid=(end_slot - first_slot, pairs),
        in_specs=[part(0), part(1), part(2), part(0)]
        + seg_specs
        + [log_spec]
        + [pl.BlockSpec(memory_space=pl.ANY)] * len(earlier),
        out_specs=[part(0), part(0), part(0)],
        out_shape=[jax.ShapeDtypeStruct((qkv.shape[0], width), jnp.bfloat16)] * 3,
        input_output_aliases={7 + idx: idx for idx in range(len(earlier))},
        cost_estimate=pl.CostEstimate(
            flops=work * 20 * HD, bytes_accessed=qkv.size * 2, transcendentals=work
        ),
    )(qkv, qkv, qkv, grad_mixed, segment[:, None, :], segment[:, :, None], log_total, *earlier)


def on_device(
    inputs,
    cotangent,
    drop_mask,
    doc_len,
    w_query,
    b_query,
    w_key,
    w_value,
    b_value,
    w_attn,
    b_attn,
    gain_one,
    shift_one,
    w_in,
    b_in,
    w_out,
    b_out,
    gain_two,
    shift_two,
):
    tok_rows = inputs[0]
    tok_count, model_width = tok_rows.shape
    slot_count = drop_mask.shape[1]
    doc_count = drop_mask.shape[2]
    seq_len = tok_count // slot_count
    my_index = lax.axis_index("dp")
    wq, bq, wk, wv, bv = (w_query[0], b_query[0], w_key[0], w_value[0], b_value[0])
    wo, bo, gone, sone = (
        w_attn[0],
        b_attn[0],
        gain_one[0].astype(jnp.float32),
        shift_one[0].astype(jnp.float32),
    )
    wi, bi, wu, bu = (w_in[0], b_in[0], w_out[0], b_out[0])
    gtwo, stwo = (gain_two[0].astype(jnp.float32), shift_two[0].astype(jnp.float32))
    ends = jnp.cumsum(doc_len[0], axis=-1)
    places = jnp.arange(seq_len, dtype=jnp.int32)
    segment = jnp.sum((places[None, :, None] >= ends[:, None, :]).astype(jnp.int32), axis=-1)
    segment = jnp.where(my_index % 2 == 0, jnp.zeros_like(segment), segment)
    chosen = segment[:, :, None] == jnp.arange(doc_count, dtype=jnp.int32)[None, None, :]
    dropped = jnp.sum(jnp.where(chosen, drop_mask[0][:, None, :], 0), axis=-1)
    keep = (dropped == 0).reshape(tok_count)
    w_three = jnp.concatenate([wq, wk, wv], axis=1)
    b_three = jnp.concatenate([bq, jnp.zeros_like(bq), bv])
    qkv = (jnp.dot(tok_rows, w_three, preferred_element_type=jnp.float32) + b_three).astype(
        jnp.bfloat16
    )
    mixed, log_total = attend(qkv, segment)
    attended = jnp.dot(mixed, wo, preferred_element_type=jnp.float32) + bo
    normed_one, scaled_one = norm_parts(tok_rows.astype(jnp.float32) + attended)
    sent = (normed_one * gone + sone).astype(jnp.bfloat16)
    grad_out = shifted(cotangent, "layer", -1)[0]
    rows_two = jnp.stack([bu.astype(jnp.float32), gtwo, stwo])
    inner, slope, layer_output, grad_outer, grad_sum, vectors_two = feed_forward(
        sent,
        wi,
        bi.astype(jnp.float32)[None],
        wu,
        rows_two,
        grad_out,
        keep.astype(jnp.float32)[:, None],
        tok_rows,
    )
    out = shifted(layer_output[None], "layer", 1)
    low_w_out, grad_outer = lax.optimization_barrier(
        (row_product(inner, grad_outer).astype(jnp.bfloat16), grad_outer)
    )
    whole_w_out = lax.psum(low_w_out, "dp")
    grad_low, grad_b_in = slope_back(grad_outer, wu, slope)
    low_w_in, grad_low = lax.optimization_barrier(
        (row_product(sent, grad_low).astype(jnp.bfloat16), grad_low)
    )
    sum_in = GroupSum(low_w_in)
    grad_sent = (back_product(grad_low, wi) + grad_sum).astype(jnp.bfloat16)
    grad_h1, grad_gain_one, grad_shift_one = norm_back(
        grad_sent.astype(jnp.float32), normed_one, scaled_one, gone
    )
    grad_attn = grad_h1.astype(jnp.bfloat16)
    grad_w_attn = row_product(mixed, grad_attn).astype(jnp.bfloat16)
    grad_b_attn = jnp.sum(grad_h1, axis=0)
    grad_mixed = back_product(grad_attn, wo).astype(jnp.bfloat16)
    early_rows = jnp.concatenate(
        [
            grad_b_in.reshape(-1, model_width),
            vectors_two[:3],
            grad_gain_one[None],
            grad_shift_one[None],
            grad_b_attn[None],
        ]
    )
    grad_mixed, grad_w_attn, early_rows = beside((grad_mixed, grad_w_attn, early_rows), sum_in)
    middle = slot_count // 2
    attention = (qkv, grad_mixed, segment, log_total)
    grads_qkv = beside(attend_back(*attention, 0, middle), sum_in)
    grads_qkv, out = beside(
        (attend_back(*attention, middle, slot_count, tuple(grads_qkv)), out), sum_in
    )
    grad_q, grad_k, grad_v = grads_qkv
    low_attention = jnp.concatenate(
        [row_product(tok_rows, grad).astype(jnp.bfloat16) for grad in grads_qkv] + [grad_w_attn],
        axis=1,
    )
    low_attention, grad_q, grad_k, grad_v = beside(
        (low_attention, grad_q, grad_k, grad_v), sum_in
    )
    sum_attention = GroupSum(low_attention)
    grad_rows = (
        back_product(grad_q, wq) + back_product(grad_k, wk) + back_product(grad_v, wv) + grad_h1
    )
    grad_inputs = jnp.where(keep[:, None], grad_rows, grad_out.astype(jnp.float32)).astype(
        jnp.bfloat16
    )
    grad_b_query = jnp.sum(grad_q.astype(jnp.float32), axis=0)
    grad_b_value = jnp.sum(grad_v.astype(jnp.float32), axis=0)
    grad_inputs, grad_b_query, grad_b_value = beside(
        (grad_inputs, grad_b_query, grad_b_value), sum_in, sum_attention
    )
    sum_rows = RowSum(
        jnp.concatenate(
            [
                early_rows,
                grad_b_query[None],
                grad_b_value[None],
            ]
        )
    )
    sum_w_out = beside(widened(whole_w_out), sum_in, sum_attention, sum_rows)
    (sum_w_in,) = beside(sum_in.placed(), sum_attention, sum_rows)
    beside((), sum_attention, sum_rows)
    rows = sum_rows.total()
    attention_sums = sum_attention.placed(4)
    sum_b_in, named = (rows[: -8].reshape(1, -1), rows[-8:])
    return (
        out,
        grad_inputs[None],
        attention_sums[0],
        named[6:7],
        attention_sums[1],
        attention_sums[2],
        named[7:8],
        attention_sums[3],
        named[5:6],
        named[3:4],
        named[4:5],
        sum_w_in,
        sum_b_in,
        sum_w_out,
        named[0:1],
        named[1:2],
        named[2:3],
    )


def solution(mesh):
    in_specs = (
        P("layer", "dp", None),
        P("layer", "dp", None),
        P("layer", "dp", None),
        P("layer", "dp", None),
        P("layer", None, None),
        P("layer", None),
        P("layer", None, None),
        P("layer", None, None),
        P("layer", None),
        P("layer", None, None),
        P("layer", None),
        P("layer", None),
        P("layer", None),
        P("layer", None, None),
        P("layer", None),
        P("layer", None, None),
        P("layer", None),
        P("layer", None),
        P("layer", None),
    )
    out_specs = (
        P("layer", "dp", None),
        P("layer", "dp", None),
        P("layer", None, None),
        P("layer", None),
        P("layer", None, None),
        P("layer", None, None),
        P("layer", None),
        P("layer", None, None),
        P("layer", None),
        P("layer", None),
        P("layer", None),
        P("layer", None, None),
        P("layer", None),
        P("layer", None, None),
        P("layer", None),
        P("layer", None),
        P("layer", None),
    )
    return jax.shard_map(
        on_device, mesh=mesh, in_specs=in_specs, out_specs=out_specs, check_vma=False
    )
```
